128 devices in a mesh: req: 16 (over z, y), mlp: 8 (over x, core).
Axes of the slice: x: 4, y: 4, z: 4, core: 2. Of those that a mesh axis runs over, the one named last changes fastest.
Arguments:
- activations: bfloat16 [8192, 4096], P('req', 'mlp')
- slot_segment: int32 [8192], P('req'), may hold values from -1 to 511, as said below
- attn_norm_gain: float32 [4096], replicated, may hold values from 0.5 to 1.5
- attn_norm_bias: float32 [4096], replicated, may hold values from -1.5 to 1.5
- mlp_norm_gain: float32 [4096], replicated, may hold values from 0.5 to 1.5
- mlp_norm_bias: float32 [4096], replicated, may hold values from -1.5 to 1.5
- qkv_weight: bfloat16 [4096, 6144], P(None, 'mlp')
- dense_weight: bfloat16 [2048, 4096], P('mlp'), may hold values from -0.1875 to 0.1875
- fc_weight: bfloat16 [4096, 8192], P(None, 'mlp'), may hold values from -0.09375 to 0.09375
- proj_weight: bfloat16 [8192, 4096], P('mlp'), may hold values from -0.09375 to 0.09375
Outputs:
- output_rows: float32 [8192, 4096], P('req', 'mlp')
- cache_rows: bfloat16 [2, 4096, 2048], P(None, 'req', 'mlp')
The draws below stay inside these ranges and needn't reach their ends.
Inputs may be any that keep to these rules, and one draw needn't show every extreme that they name: `slot_segment`: each group's 512 slots hold live slots first and -1 after them; the live count of every group is a multiple of 16 between 16 and 512, the counts of all groups sum to 4096, and some group is full, its last slot beginning a prompt of one token. A live slot holds the group slot where its prompt begins; a prompt's slots are consecutive.
All inputs are finite; a program needn't handle non-finite values.
Results may differ from the reference program's by a relative error of at most 0.0047.
The reference program's roundings to bfloat16 on the way count: a program that leaves them out, or rounds other values in their place, can miss the bound.
Values may be sent and summed in bfloat16 or wider, within the bound.
A program may use at most 128 MiB of HBM per device.

```python
import math
import jax
import jax.numpy as jnp
from jax import lax

D = 4096
HEADS = 16
HD = 128
ROT = 32
FF = 8192
SLOTS = 512
LIVE_DEV = 256
N_REQ = 16
N_MLP = 8


def draw_activations(key, part):
    draw_keys = jax.random.split(jax.random.fold_in(key, 3), 3)
    row_total = N_REQ * SLOTS
    row_scale = jnp.exp(jax.random.uniform(draw_keys[0], (row_total, 1), jnp.float32) * math.log(10.0))
    col_scale = jnp.exp((jax.random.uniform(draw_keys[1], (1, D), jnp.float32) - 0.5) * math.log(10.0))
    values = jax.random.normal(draw_keys[2], (row_total, D), jnp.float32) * row_scale * col_scale
    return values.astype(jnp.bfloat16)


def draw_qkv_weight(key, part):
    draw_keys = jax.random.split(jax.random.fold_in(key, 11), 4)
    base = jax.random.normal(draw_keys[0], (D, HEADS, HD), jnp.float32)
    query_part = base
    key_part = jax.random.normal(draw_keys[2], (D, HEADS, HD), jnp.float32)
    value_part = jax.random.normal(draw_keys[3], (D, HEADS, HD), jnp.float32)
    stacked = jnp.stack([query_part, key_part, value_part], axis=2).reshape(D, HEADS * 3 * HD)
    return (stacked * D ** (-0.5)).astype(jnp.bfloat16)


def draw_slot_segment(key, part):
    draw_keys = jax.random.split(jax.random.fold_in(key, 5), 3)
    per_peer = SLOTS // N_REQ
    full_group = jax.random.randint(draw_keys[0], (), 0, N_REQ)
    extra = LIVE_DEV - per_peer - (N_REQ - 1)
    pool_size = (N_REQ - 1) * (per_peer - 1)
    order = jax.random.permutation(draw_keys[1], pool_size)
    chosen = order < extra
    owner = jnp.arange(pool_size, dtype=jnp.int32) // (per_peer - 1)
    counts = jnp.sum((owner[None, :] == jnp.arange(N_REQ - 1, dtype=jnp.int32)[:, None]) & chosen[None, :], axis=1)
    other_units = (1 + counts).astype(jnp.int32)
    group_index = jnp.arange(N_REQ, dtype=jnp.int32)
    other_pos = jnp.clip(group_index - (group_index > full_group).astype(jnp.int32), 0, N_REQ - 2)
    group_units = jnp.where(group_index == full_group, per_peer, other_units[other_pos])
    group_fill = group_units * N_REQ
    slot_index = jnp.arange(SLOTS, dtype=jnp.int32)
    last_start = (group_index[:, None] == full_group) & (slot_index[None, :] == SLOTS - 1)
    starts = (jax.random.randint(draw_keys[2], (N_REQ, SLOTS), 0, 40) == 0) | (slot_index[None, :] == 0) | last_start
    first_slot = lax.cummax(jnp.where(starts, slot_index[None, :], 0), axis=1)
    segment = jnp.where(slot_index[None, :] < group_fill[:, None], first_slot, -1)
    return segment.reshape(-1).astype(jnp.int32)


def strengthened(values, key, source, target, shards_of, factor):
    def block_of(dim):
        return (jnp.arange(values.shape[dim]) // (values.shape[dim] // shards_of)).reshape((-1,) + (1,) * (values.ndim - 1 - dim))

    one_side = jax.random.permutation(key, shards_of)[block_of(target)]
    far = (block_of(target) + shards_of // 2) % shards_of
    return jnp.where((block_of(source) == one_side) | (block_of(source) == far), factor * values, values)


def steps_of(rng, shape, pieces, least, largest):
    def one(dim, shards_of):
        heights = jax.random.uniform(jax.random.fold_in(jax.random.fold_in(rng, 6), dim), (shards_of,), jnp.float32, least / len(pieces), largest / len(pieces))
        return jnp.repeat(jnp.exp(heights), shape[dim] // shards_of).reshape((-1,) + (1,) * (len(shape) - dim - 1))

    loudness = one(*pieces[0])
    for cut in pieces[1:]:
        loudness = loudness * one(*cut)
    return loudness


def bell_draw(own_key, extent, scale, limit, shards=(), kind=jnp.bfloat16):
    loudness = steps_of(own_key, extent, shards, -0.22, 0.18) if shards else 1.0
    drawn = jax.random.normal(own_key, extent, jnp.float32) * scale * loudness
    return jnp.minimum(jnp.maximum(drawn, -limit), limit).astype(kind)


def heavy_noise(rng, dims, deviation, most, pieces, heavy, kind=jnp.bfloat16):
    array = deviation * jax.random.normal(rng, dims, jnp.float32)
    if pieces:
        array = array * steps_of(rng, dims, pieces, -0.22, 0.18)
    return jnp.clip(strengthened(array, jax.random.fold_in(rng, 3), *heavy), -most, most).astype(kind)


def setup_inputs(seed: int = 0) -> dict:
    keys = jax.random.split(jax.random.key(seed), 11)
    activations = draw_activations(jax.random.fold_in(keys[10], 71), 0)
    slot_segment = draw_slot_segment(jax.random.fold_in(keys[10], 71), 0)
    attn_norm_gain = jnp.clip(1.0 + 0.1 * jax.random.normal(keys[2], (D,), jnp.float32), 0.5, 1.5)
    attn_norm_bias = bell_draw(keys[3], (D,), 0.3, 1.5, (), jnp.float32)
    mlp_norm_gain = jnp.clip(1.0 + 0.1 * jax.random.normal(keys[4], (D,), jnp.float32), 0.5, 1.5)
    mlp_norm_bias = bell_draw(keys[5], (D,), 0.3, 1.5, (), jnp.float32)
    qkv_weight = draw_qkv_weight(jax.random.fold_in(keys[10], 71), 0)
    dense_weight = heavy_noise(keys[7], (HEADS * HD, D), (HEADS * HD) ** -0.5, 0.1875, ((0, 8),), (0, 1, 8, 2.0))
    fc_weight = bell_draw(keys[8], (D, FF), D ** -0.5, 0.09375, ((1, 8),))
    proj_weight = heavy_noise(keys[9], (FF, D), FF ** -0.5, 0.09375, ((0, 8),), (0, 1, 8, 2.0))
    return dict(activations=activations, slot_segment=slot_segment, attn_norm_gain=attn_norm_gain, attn_norm_bias=attn_norm_bias, mlp_norm_gain=mlp_norm_gain, mlp_norm_bias=mlp_norm_bias, qkv_weight=qkv_weight, dense_weight=dense_weight, fc_weight=fc_weight, proj_weight=proj_weight)


def layer_norm(row_data, gain_vec, bias_vec):
    row_data = row_data.astype(jnp.float32)
    row_mean = lax.optimization_barrier(jnp.mean(row_data, axis=-1, keepdims=True))
    centered = row_data - row_mean
    variance = lax.optimization_barrier(jnp.mean(centered * centered, axis=-1, keepdims=True))
    return (centered * lax.rsqrt(variance + 1e-05) * gain_vec + bias_vec).astype(jnp.bfloat16)

def rotate(head_data, position):
    half_rot = ROT // 2
    inv_freq = 10000.0 ** (-(jnp.arange(half_rot).astype(jnp.float32) * 2.0 / ROT))
    angles = position.astype(jnp.float32)[:, None] * inv_freq[None, :]
    cosine = jnp.concatenate([jnp.cos(angles), jnp.cos(angles)], axis=-1)[:, None, :]
    sine_part = jnp.concatenate([jnp.sin(angles), jnp.sin(angles)], axis=-1)[:, None, :]
    rot_part = head_data[..., :ROT]
    pass_part = head_data[..., ROT:]
    first_half = rot_part[..., :half_rot]
    second = rot_part[..., half_rot:]
    turned = jnp.concatenate([-second, first_half], axis=-1)
    return jnp.concatenate([rot_part * cosine + turned * sine_part, pass_part], axis=-1)

def attend(normed, segment, qkv_weight):
    slot_count = normed.shape[0]
    head_count = qkv_weight.shape[1] // (3 * HD)
    mixed_proj = jnp.dot(normed, qkv_weight, preferred_element_type=jnp.float32).reshape(slot_count, head_count, 3, HD)
    slot_index = jnp.arange(slot_count, dtype=jnp.int32)
    position = slot_index - segment
    query_rows = rotate(mixed_proj[:, :, 0], position).astype(jnp.bfloat16)
    key_rows = rotate(mixed_proj[:, :, 1], position).astype(jnp.bfloat16)
    value_rows = mixed_proj[:, :, 2].astype(jnp.bfloat16)
    scores = jnp.einsum('qhd,khd->hqk', query_rows.astype(jnp.float32), key_rows.astype(jnp.float32)) * HD ** (-0.5)
    allowed = (segment[:, None] == segment[None, :]) & (slot_index[None, :] <= slot_index[:, None]) & (segment[:, None] >= 0)
    scores = jnp.where(allowed[None], scores, -1e+30)
    row_max = lax.optimization_barrier(jnp.max(scores, axis=-1, keepdims=True))
    weights = jnp.exp(scores - row_max)
    prob_rows = (weights / lax.optimization_barrier(jnp.sum(weights, axis=-1, keepdims=True))).astype(jnp.bfloat16)
    context = jnp.einsum('hqk,khd->qhd', prob_rows.astype(jnp.float32), value_rows.astype(jnp.float32))
    context = context.astype(jnp.bfloat16).reshape(slot_count, head_count * HD)
    return (context, key_rows.reshape(slot_count, head_count * HD), value_rows.reshape(slot_count, head_count * HD))

def grouped_sum(left_rows, right_rows, group_count):
    group_width = left_rows.shape[1] // group_count
    running = jnp.zeros((left_rows.shape[0], right_rows.shape[1]), jnp.float32)
    for member in range(group_count):
        term = jnp.dot(left_rows[:, member * group_width:(member + 1) * group_width], right_rows[member * group_width:(member + 1) * group_width], preferred_element_type=jnp.float32)
        running = running + lax.optimization_barrier(term.astype(jnp.bfloat16)).astype(jnp.float32)
    return running

def reference(activations, slot_segment, attn_norm_gain, attn_norm_bias, mlp_norm_gain, mlp_norm_bias, qkv_weight, dense_weight, fc_weight, proj_weight):
    group_rows = activations.reshape(N_REQ, SLOTS, D)
    group_segs = slot_segment.reshape(N_REQ, SLOTS)

    def one_group(inputs):
        row_block, segment = inputs
        normed = layer_norm(row_block, attn_norm_gain, attn_norm_bias)
        context, key_rows, value_rows = attend(normed, segment, qkv_weight)
        branch = grouped_sum(context, dense_weight, N_MLP)
        return (branch, key_rows, value_rows)
    attn_branch, all_keys, values = lax.map(one_group, (group_rows, group_segs))
    live_slot = group_segs >= 0
    group_units = (lax.optimization_barrier(jnp.sum(live_slot.astype(jnp.int32), axis=1)) // N_REQ).astype(jnp.int32)
    offset = (jnp.cumsum(group_units) - group_units).astype(jnp.int32)
    slot_index = jnp.arange(SLOTS, dtype=jnp.int32)
    dest_row = (slot_index % N_REQ)[None, :] * LIVE_DEV + offset[:, None] + (slot_index // N_REQ)[None, :]
    dest_row = jnp.where(live_slot, dest_row, N_REQ * LIVE_DEV).astype(jnp.int32)
    source = jnp.zeros((N_REQ * LIVE_DEV,), jnp.int32).at[dest_row.reshape(-1)].set(jnp.arange(N_REQ * SLOTS, dtype=jnp.int32), mode='drop')
    flat_rows = activations.reshape(N_REQ * SLOTS, D)
    even_rows = flat_rows[source]
    normed = layer_norm(even_rows, mlp_norm_gain, mlp_norm_bias)
    hidden = jax.nn.gelu(jnp.dot(normed, fc_weight, preferred_element_type=jnp.float32), approximate=False)
    hidden = hidden.astype(jnp.bfloat16)
    mlp_rows = grouped_sum(hidden, proj_weight, N_MLP)
    mlp_branch = jnp.zeros((N_REQ * SLOTS, D), jnp.float32).at[source].set(mlp_rows)
    combined = flat_rows.astype(jnp.float32) + attn_branch.reshape(N_REQ * SLOTS, D) + mlp_branch
    output_rows = jnp.where(live_slot.reshape(-1)[:, None], combined, 0.0).astype(jnp.float32)
    width_all = HEADS * HD
    cache_rows = jnp.stack([all_keys.reshape(-1, width_all)[source], values.reshape(-1, width_all)[source]])
    return (output_rows, cache_rows)
```

```python
import jax
import jax.numpy as jnp
from jax import lax
from jax.sharding import PartitionSpec as P

HD = 128
ROT = 32
LIVE_DEV = 256


def layer_norm(row_data, gain_vec, bias_vec):
    row_data = row_data.astype(jnp.float32)
    row_mean = jnp.mean(row_data, axis=-1, keepdims=True)
    centered = row_data - row_mean
    variance = jnp.mean(centered * centered, axis=-1, keepdims=True)
    return (centered * lax.rsqrt(variance + 1e-05) * gain_vec + bias_vec).astype(jnp.bfloat16)


def rotate(head_data, position):
    half_rot = ROT // 2
    inv_freq = 10000.0 ** (-(jnp.arange(half_rot).astype(jnp.float32) * 2.0 / ROT))
    angles = position.astype(jnp.float32)[:, None] * inv_freq[None, :]
    cosine = jnp.concatenate([jnp.cos(angles), jnp.cos(angles)], axis=-1)[:, None, :]
    sine_part = jnp.concatenate([jnp.sin(angles), jnp.sin(angles)], axis=-1)[:, None, :]
    rot_part = head_data[..., :ROT]
    pass_part = head_data[..., ROT:]
    first_half = rot_part[..., :half_rot]
    second = rot_part[..., half_rot:]
    turned = jnp.concatenate([-second, first_half], axis=-1)
    return jnp.concatenate([rot_part * cosine + turned * sine_part, pass_part], axis=-1)


def attend(normed, segment, qkv_weight):
    slot_count = normed.shape[0]
    head_count = qkv_weight.shape[1] // (3 * HD)
    mixed_proj = jnp.dot(normed, qkv_weight, preferred_element_type=jnp.float32).reshape(
        slot_count, head_count, 3, HD
    )
    slot_index = jnp.arange(slot_count, dtype=jnp.int32)
    position = slot_index - segment
    query_rows = rotate(mixed_proj[:, :, 0], position).astype(jnp.bfloat16)
    key_rows = rotate(mixed_proj[:, :, 1], position).astype(jnp.bfloat16)
    value_rows = mixed_proj[:, :, 2].astype(jnp.bfloat16)
    scores = jnp.einsum(
        "qhd,khd->hqk", query_rows, key_rows, preferred_element_type=jnp.float32
    ) * HD ** (-0.5)
    allowed = (
        (segment[:, None] == segment[None, :])
        & (slot_index[None, :] <= slot_index[:, None])
        & (segment[:, None] >= 0)
    )
    scores = jnp.where(allowed[None], scores, -1e30)
    row_max = jnp.max(scores, axis=-1, keepdims=True)
    weights = jnp.exp(scores - row_max)
    prob_rows = (weights / jnp.sum(weights, axis=-1, keepdims=True)).astype(jnp.bfloat16)
    context = jnp.einsum("hqk,khd->qhd", prob_rows, value_rows, preferred_element_type=jnp.float32)
    context = context.astype(jnp.bfloat16).reshape(slot_count, head_count * HD)
    return (
        context,
        key_rows.reshape(slot_count, head_count * HD),
        value_rows.reshape(slot_count, head_count * HD),
    )


def body(
    activations,
    slot_segment,
    attn_norm_gain,
    attn_norm_bias,
    mlp_norm_gain,
    mlp_norm_bias,
    qkv_weight,
    dense_weight,
    fc_weight,
    proj_weight,
):
    slot_count = activations.shape[0]
    groups = lax.axis_size("req")
    per_peer = slot_count // groups
    live_slot = slot_segment >= 0
    group_fill = lax.all_gather(
        jnp.sum(live_slot.astype(jnp.int32)).reshape(1), "req", axis=0, tiled=True
    )
    group_units = group_fill // groups
    received_live = (jnp.arange(per_peer, dtype=jnp.int32)[None, :] < group_units[:, None]).reshape(
        -1
    )
    live_rank = jnp.cumsum(received_live.astype(jnp.int32)) - 1
    target = jnp.where(received_live, live_rank, LIVE_DEV)
    pick_rows = (
        jnp.zeros((LIVE_DEV,), jnp.int32)
        .at[target]
        .set(jnp.arange(groups * per_peer, dtype=jnp.int32), mode="drop")
    )
    full_rows = lax.all_gather(activations, "mlp", axis=1, tiled=True)
    normed = layer_norm(full_rows, attn_norm_gain, attn_norm_bias)
    context, key_rows, value_rows = attend(normed, slot_segment, qkv_weight)
    key_value = jnp.concatenate([key_rows, value_rows], axis=1).reshape(per_peer, groups, -1)
    cache_rows = lax.all_to_all(key_value, "req", split_axis=1, concat_axis=0, tiled=True)
    cache_rows = jnp.take(cache_rows.reshape(groups * per_peer, -1), pick_rows, axis=0)
    width = key_rows.shape[1]
    cache_rows = jnp.stack([cache_rows[:, :width], cache_rows[:, width:]])
    mlp_normed = layer_norm(full_rows, mlp_norm_gain, mlp_norm_bias)
    hidden = jax.nn.gelu(
        jnp.dot(mlp_normed, fc_weight, preferred_element_type=jnp.float32), approximate=False
    )
    hidden = hidden.astype(jnp.bfloat16)
    part = jnp.dot(context, dense_weight, preferred_element_type=jnp.float32) + jnp.dot(
        hidden, proj_weight, preferred_element_type=jnp.float32
    )
    total = lax.psum_scatter(
        part.astype(jnp.bfloat16), "mlp", scatter_dimension=1, tiled=True
    ).astype(jnp.float32)
    combined = activations.astype(jnp.float32) + total
    output_rows = jnp.where(live_slot[:, None], combined, 0.0)
    return (output_rows, cache_rows)


def solution(mesh):
    placed = (
        P("req", "mlp"),
        P("req"),
        P(),
        P(),
        P(),
        P(),
        P(None, "mlp"),
        P("mlp", None),
        P(None, "mlp"),
        P("mlp", None),
    )
    return jax.shard_map(
        body,
        mesh=mesh,
        in_specs=placed,
        out_specs=(P("req", "mlp"), P(None, "req", "mlp")),
        check_vma=False,
    )
```

```python
import functools
import math

import jax
import jax.numpy as jnp
from jax import lax
from jax.experimental import pallas as pl
from jax.experimental.pallas import tpu as pltpu
from jax.sharding import PartitionSpec as P

HD = 128
ROT = 32
F32 = jnp.float32
BF16 = jnp.bfloat16
MESH = pl.DeviceIdType.MESH

LA, LB, OA, RA, RB, OB, PP, PL, PR, POA, POB = range(11)
OWN, RIGHT, OPP, LEFT = 0, 1, 2, 3


def remote(src, dst, send_sem, recv_sem, dev):
    return pltpu.make_async_remote_copy(
        src_ref=src,
        dst_ref=dst,
        send_sem=send_sem,
        recv_sem=recv_sem,
        device_id=dev,
        device_id_type=MESH,
    )


def layer_kernel(
    groups,
    members,
    act,
    seg,
    g1,
    b1,
    g2,
    b2,
    wq_h,
    wd_h,
    wf_h,
    wp_h,
    out,
    cache,
    xf,
    wq,
    wf,
    wo,
    n1,
    n2,
    gs,
    segc,
    tab,
    qb,
    kvb,
    hc,
    kvp,
    kvr,
    cnt_s,
    cnt_r,
    psend,
    precv,
    mine,
    lo_s,
    lo_r,
    lb_s,
    lb_r,
    wsem,
    lsem,
    ag_ss,
    ag_rs,
    kv_ss,
    kv_rs,
    ct_ss,
    ct_rs,
    p_ss,
    p_rs,
    lo_ss,
    lo_rs,
    lb_ss,
    lb_rs,
):
    rows = xf.shape[2]
    half = rows // 2
    width = xf.shape[3]
    chips = members // 2
    model = members * width
    heads = qb.shape[1] // HD
    kv_w = heads * HD
    per_peer = kvp.shape[0] // groups
    me_g = lax.axis_index("req")
    me = lax.axis_index("mlp")
    core = lax.rem(me, 2)
    chip = me // 2
    right = lax.rem(me + 2, members)
    left = lax.rem(me + members - 2, members)
    opp = lax.rem(me + members // 2, members)
    flip = 1 - 2 * core
    partner = me + flip
    to_right, to_left, to_partner = (me_g, right), (me_g, left), (me_g, partner)

    copies = [
        pltpu.make_async_copy(wq_h, wq, wsem.at[0]),
        pltpu.make_async_copy(wf_h, wf, wsem.at[1]),
        pltpu.make_async_copy(wd_h, wo.at[pl.ds(0, kv_w)], wsem.at[2]),
        pltpu.make_async_copy(wp_h, wo.at[pl.ds(kv_w, wo.shape[0] - kv_w)], wsem.at[3]),
    ]
    own_copies = [
        pltpu.make_async_copy(act.at[pl.ds(h * rows, rows)], xf.at[h, me], lsem.at[h])
        for h in range(2)
    ]

    barrier = pltpu.get_barrier_semaphore()
    for dev in (to_right, to_left, to_partner):
        pl.semaphore_signal(barrier, inc=1, device_id=dev, device_id_type=MESH)

    def greet(t, carry):
        peer = lax.rem(me_g + t, groups)
        pl.semaphore_signal(barrier, inc=1, device_id=(peer, me), device_id_type=MESH)
        return carry

    lax.fori_loop(1, groups, greet, 0)
    for c in own_copies + copies:
        c.start()
    pl.semaphore_wait(barrier, 3 + groups - 1)

    lo_rows, hi_rows = pl.ds(0, half), pl.ds(half, half)

    def ag(h, kind, src, dst, dev):
        return remote(src, dst, ag_ss.at[h, kind], ag_rs.at[h, kind], dev)

    def got(h, kind, ref):
        remote(ref, ref, ag_ss.at[h, kind], ag_rs.at[h, kind], to_partner).wait_recv()

    sent = []

    def go(copy):
        copy.start()
        sent.append(copy)

    def gather_own(h):
        a = act.at[pl.ds(h * rows, half)]
        b = act.at[pl.ds(h * rows + half, half)]
        go(ag(h, LA, a, xf.at[h, me, lo_rows], to_right))
        go(ag(h, RB, b, xf.at[h, me, hi_rows], to_left))
        go(ag(h, LB, b, xf.at[h, me, hi_rows], to_right))
        go(ag(h, RA, a, xf.at[h, me, lo_rows], to_left))
        go(ag(h, PP, act.at[pl.ds(h * rows, rows)], xf.at[h, me], to_partner))

    def gather_far(h):
        got(h, LA, xf.at[h, left, lo_rows])
        go(ag(h, OA, xf.at[h, left, lo_rows], xf.at[h, left, lo_rows], to_right))
        got(h, RB, xf.at[h, right, hi_rows])
        go(ag(h, OB, xf.at[h, right, hi_rows], xf.at[h, right, hi_rows], to_left))

    def gather_near(h):
        got(h, LB, xf.at[h, left, hi_rows])
        go(ag(h, PL, xf.at[h, left], xf.at[h, left], to_partner))
        got(h, RA, xf.at[h, right, lo_rows])
        go(ag(h, PR, xf.at[h, right], xf.at[h, right], to_partner))

    def gather_opp(h):
        got(h, OA, xf.at[h, opp, lo_rows])
        go(ag(h, POA, xf.at[h, opp, lo_rows], xf.at[h, opp, lo_rows], to_partner))
        got(h, OB, xf.at[h, opp, hi_rows])
        go(ag(h, POB, xf.at[h, opp, hi_rows], xf.at[h, opp, hi_rows], to_partner))

    def gather_end(h):
        own_copies[h].wait()
        got(h, PP, xf.at[h, partner])
        got(h, PL, xf.at[h, left + flip])
        got(h, PR, xf.at[h, right + flip])
        got(h, POA, xf.at[h, opp + flip, lo_rows])
        got(h, POB, xf.at[h, opp + flip, hi_rows])

    gather_own(0)

    for i, ref in enumerate((g1, b1, g2, b2)):
        for m in range(members):
            for t in range(width // 128):
                k = m * (width // 128) + t
                gs[i, m : m + 1, t * 128 : (t + 1) * 128] = ref[k : k + 1, :]
    live_sum = jnp.sum((seg[...] >= 0).astype(F32), axis=1, keepdims=True)
    units = jnp.sum(live_sum, axis=0, keepdims=True) * (1.0 / groups)
    cnt_s[...] = jnp.broadcast_to(units, cnt_s.shape)
    for b in range(seg.shape[0]):
        block = jnp.broadcast_to(seg[b : b + 1, :].astype(F32), (128, 128))
        segc[b * 128 : (b + 1) * 128, :] = block.T

    lane = lax.broadcasted_iota(jnp.int32, (128, 128), 1)
    pair = lax.rem(lane, ROT // 2).astype(F32)
    freq = jnp.where(lane < ROT, jnp.exp(pair * (-2.0 / ROT * math.log(10000.0))), 0.0)

    def angles(b, carry):
        at = pl.ds(pl.multiple_of(b * 128, 128), 128)
        slot = (b * 128 + lax.broadcasted_iota(jnp.int32, (128, 128), 0)).astype(F32)
        ang = (slot - segc[at, :]) * freq
        sine = jnp.sin(ang)
        tab[0, at, :] = jnp.cos(ang)
        tab[1, at, :] = jnp.where(lane < ROT // 2, -sine, 0.0)
        tab[2, at, :] = jnp.where(lane < ROT // 2, 0.0, sine)
        return carry

    gather_far(0)
    gather_own(1)
    lax.fori_loop(0, seg.shape[0], angles, 0)
    gather_near(0)
    gather_opp(0)

    def count_out(t, carry):
        peer = lax.rem(me_g + t, groups)
        remote(cnt_s, cnt_r.at[me_g], ct_ss.at[t], ct_rs.at[t], (peer, me)).start()
        return carry

    lax.fori_loop(1, groups, count_out, 0)

    def norms(h):
        def body(r, carry):
            at = pl.ds(pl.multiple_of(r * 16, 16), 16)
            xs = [xf[h, m, at, :].astype(F32) for m in range(members)]
            total = functools.reduce(lambda a, b: a + b, xs)
            mean = jnp.sum(total, axis=-1, keepdims=True) * (1.0 / model)
            cs = [x - mean for x in xs]
            square = functools.reduce(lambda a, b: a + b, [c * c for c in cs])
            scale = lax.rsqrt(jnp.sum(square, axis=-1, keepdims=True) * (1.0 / model) + 1e-05)
            for m in range(members):
                y = cs[m] * scale
                cols = slice(m * width, (m + 1) * width)
                n1[at, cols] = (y * gs[0, m : m + 1, :] + gs[1, m : m + 1, :]).astype(BF16)
                n2[at, cols] = (y * gs[2, m : m + 1, :] + gs[3, m : m + 1, :]).astype(BF16)
            return carry

        lax.fori_loop(0, rows // 16, body, 0)

    def project(h):
        at = slice(h * rows, (h + 1) * rows)
        parts = []
        for n in range(wq.shape[1] // 256):
            acc = jnp.dot(n1[...], wq[:, n * 256 : (n + 1) * 256], preferred_element_type=F32)
            parts += [acc[:, :HD], acc[:, HD:]]
        cos, s1, s2 = tab[0, at, :], tab[1, at, :], tab[2, at, :]

        def turn(u):
            return u * cos + pltpu.roll(u, HD - ROT // 2, 1) * s1 + pltpu.roll(u, ROT // 2, 1) * s2

        for i in range(heads):
            cols = slice(i * HD, (i + 1) * HD)
            qb[:, cols] = turn(parts[3 * i]).astype(BF16)
            kvb[at, cols] = turn(parts[3 * i + 1]).astype(BF16)
            kvb[at, kv_w + i * HD : kv_w + (i + 1) * HD] = parts[3 * i + 2].astype(BF16)

    def attend(h):
        keys = (h + 1) * rows
        first = jnp.concatenate([segc[h * rows : (h + 1) * rows, :]] * (keys // 128), axis=1)
        query = (h * rows + lax.broadcasted_iota(jnp.int32, (rows, keys), 0)).astype(F32)
        key = lax.broadcasted_iota(jnp.int32, (rows, keys), 1).astype(F32)
        allowed = (key >= first) & (key <= query)
        for i in range(heads):
            cols = slice(i * HD, (i + 1) * HD)
            s = lax.dot_general(
                qb[:, cols],
                kvb[0:keys, cols],
                (((1,), (1,)), ((), ())),
                preferred_element_type=F32,
            ) * (HD**-0.5)
            s = jnp.where(allowed, s, -1e30)
            w = jnp.exp(s - jnp.max(s, axis=-1, keepdims=True))
            p = (w / jnp.sum(w, axis=-1, keepdims=True)).astype(BF16)
            ctx = jnp.dot(
                p, kvb[0:keys, kv_w + i * HD : kv_w + (i + 1) * HD], preferred_element_type=F32
            )
            hc[:, cols] = ctx.astype(BF16)

    def expand(h):
        for n in range(wf.shape[1] // 256):
            cols = slice(n * 256, (n + 1) * 256)
            u = jnp.dot(n2[...], wf[:, cols], preferred_element_type=F32)
            u = 0.5 * u * (1.0 + lax.erf(u * (0.5**0.5)))
            hc[:, kv_w + n * 256 : kv_w + (n + 1) * 256] = u.astype(BF16)

    def pcopy(h, rel):
        return remote(psend.at[h, rel], precv.at[h, rel], p_ss.at[h, rel], p_rs.at[h, rel], to_partner)

    def contract(h, rel):
        block = 2 * lax.rem(chip + rel, chips)
        for theirs in (True, False):
            col = (block + (1 - core if theirs else core)) * width
            acc = jnp.dot(
                hc[...],
                wo[:, pl.ds(pl.multiple_of(col, width), width)],
                preferred_element_type=F32,
            )
            if theirs:
                psend[h, rel] = acc.astype(BF16)
                go(pcopy(h, rel))
            else:
                mine[h, rel] = acc

    def chip_sum(h, rel, at=slice(None)):
        return mine[h, rel, at, :] + precv[h, rel, at, :].astype(F32)

    def low(h, way):
        dev = to_right if way == 0 else to_left
        return remote(lo_s.at[h, way], lo_r.at[h, way], lo_ss.at[h, way], lo_rs.at[h, way], dev)

    def back(h, way, piece):
        dev = to_right if way == 0 else to_left
        return remote(
            lb_s.at[h, way, piece],
            lb_r.at[h, way, piece],
            lb_ss.at[h, way, piece],
            lb_rs.at[h, way, piece],
            dev,
        )

    top, bottom = slice(0, half), slice(half, rows)

    def scatter_opp(h):
        pcopy(h, OPP).wait_recv()
        lo_s[h, 0] = chip_sum(h, OPP, top).astype(BF16)
        go(low(h, 0))
        lo_s[h, 1] = chip_sum(h, OPP, bottom).astype(BF16)
        go(low(h, 1))

    def scatter_near(h, way):
        rel = RIGHT if way == 0 else LEFT
        piece = 1 - way
        pcopy(h, rel).wait_recv()
        lb_s[h, way, piece] = chip_sum(h, rel, (top, bottom)[piece]).astype(BF16)
        go(back(h, way, piece))

    def scatter_far(h):
        for way in range(2):
            rel = RIGHT if way == 0 else LEFT
            piece = way
            low(h, way).wait_recv()
            total = chip_sum(h, rel, (top, bottom)[piece]) + lo_r[h, way].astype(F32)
            lb_s[h, way, piece] = total.astype(BF16)
            go(back(h, way, piece))

    def finish(h):
        pcopy(h, OWN).wait_recv()
        for piece in range(2):
            for way in range(2):
                back(h, way, piece).wait_recv()
            at = (top, bottom)[piece]
            total = chip_sum(h, OWN, at)
            total = total + lb_r[h, 0, piece].astype(F32) + lb_r[h, 1, piece].astype(F32)
            base = h * rows + piece * half
            x = xf[h, me, at, :].astype(F32)
            first = jnp.concatenate([segc[base : base + half, :]] * (width // 128), axis=1)
            out[base : base + half, :] = jnp.where(first >= 0.0, x + total, 0.0)

    def cache_out():
        slots = kvp.shape[0]
        r = lax.broadcasted_iota(jnp.int32, (slots, slots), 0)
        s = lax.broadcasted_iota(jnp.int32, (slots, slots), 1)
        pick = s == lax.rem(r, per_peer) * groups + r // per_peer
        pick = jnp.where(pick, 1.0, 0.0).astype(BF16)
        kvp[...] = jnp.dot(pick, kvb[...], preferred_element_type=F32).astype(BF16)

        def body(t, carry):
            peer = lax.rem(me_g + t, groups)
            kv_copy(t, peer).start()
            return carry

        lax.fori_loop(1, groups, body, 0)

    def kv_copy(t, peer):
        src = kvp.at[pl.ds(pl.multiple_of(peer * per_peer, per_peer), per_peer)]
        dst = kvr.at[pl.ds(pl.multiple_of(me_g * per_peer, per_peer), per_peer)]
        return remote(src, dst, kv_ss.at[t], kv_rs.at[t], (peer, me))

    def cache_in():
        here = pl.ds(pl.multiple_of(me_g * per_peer, per_peer), per_peer)
        kvr[here, :] = kvp[here, :]
        cnt_r[me_g] = cnt_s[...]

        def body(t, carry):
            peer = lax.rem(me_g + groups - t, groups)
            from_peer = pl.ds(pl.multiple_of(peer * per_peer, per_peer), per_peer)
            dst = kvr.at[from_peer]
            remote(dst, dst, kv_ss.at[t], kv_rs.at[t], (peer, me)).wait_recv()
            dst = cnt_r.at[peer]
            remote(dst, dst, ct_ss.at[t], ct_rs.at[t], (peer, me)).wait_recv()
            return carry

        lax.fori_loop(1, groups, body, 0)
        per_block = 128 // per_peer
        live_rows = cache.shape[1]
        row = lax.broadcasted_iota(jnp.int32, (live_rows, 128), 0).astype(F32)
        lane1 = lax.broadcasted_iota(jnp.int32, (1, 128), 1)
        owner = lane1 // per_peer
        unit = lax.rem(lane1, per_peer).astype(F32)
        before = jnp.zeros((1, 128), F32)
        acc = jnp.zeros((live_rows, kvr.shape[1]), F32)
        for b in range(groups // per_block):
            have = jnp.zeros((1, 128), F32)
            start = jnp.zeros((1, 128), F32)
            for t in range(per_block):
                count = cnt_r[b * per_block + t, 0:1, :]
                have = jnp.where(owner == t, count, have)
                start = jnp.where(owner == t, before, start)
                before = before + count
            place = jnp.where(unit < have, start + unit, -1.0)
            pick = jnp.where(row == place, 1.0, 0.0).astype(BF16)
            acc = acc + jnp.dot(
                pick, kvr[b * 128 : (b + 1) * 128, :], preferred_element_type=F32
            )
        cache[0] = acc[:, :kv_w].astype(BF16)
        cache[1] = acc[:, kv_w:].astype(BF16)

    gather_end(0)
    norms(0)
    copies[0].wait()
    project(0)
    gather_far(1)
    attend(0)
    copies[1].wait()
    expand(0)
    gather_near(1)
    copies[2].wait()
    copies[3].wait()
    contract(0, OPP)
    contract(0, RIGHT)
    gather_opp(1)
    scatter_opp(0)
    contract(0, LEFT)
    scatter_near(0, 0)
    contract(0, OWN)
    scatter_near(0, 1)
    gather_end(1)
    norms(1)
    scatter_far(0)
    project(1)
    cache_out()
    attend(1)
    expand(1)
    contract(1, OPP)
    contract(1, RIGHT)
    scatter_opp(1)
    contract(1, LEFT)
    scatter_near(1, 0)
    contract(1, OWN)
    scatter_near(1, 1)
    finish(0)
    cache_in()
    scatter_far(1)
    finish(1)

    for copy in sent:
        copy.wait_send()

    def drain(t, carry):
        peer = lax.rem(me_g + t, groups)
        kv_copy(t, peer).wait_send()
        remote(cnt_s, cnt_r.at[me_g], ct_ss.at[t], ct_rs.at[t], (peer, me)).wait_send()
        return carry

    lax.fori_loop(1, groups, drain, 0)


def body(
    activations,
    slot_segment,
    attn_norm_gain,
    attn_norm_bias,
    mlp_norm_gain,
    mlp_norm_bias,
    qkv_weight,
    dense_weight,
    fc_weight,
    proj_weight,
):
    slots, width = activations.shape
    groups = lax.axis_size("req")
    members = lax.axis_size("mlp")
    model = qkv_weight.shape[0]
    rows = slots // 2
    half = rows // 2
    kv_w = dense_weight.shape[0]
    ff = fc_weight.shape[1]
    live_rows = slots // 2
    chips = members // 2
    dma = pltpu.SemaphoreType.DMA
    any_spec = pl.BlockSpec(memory_space=pl.ANY)
    vmem_spec = pl.BlockSpec(memory_space=pltpu.VMEM)
    vecs = [
        v.reshape(model // 128, 128)
        for v in (attn_norm_gain, attn_norm_bias, mlp_norm_gain, mlp_norm_bias)
    ]
    return pl.pallas_call(
        functools.partial(layer_kernel, groups, members),
        name="layer",
        out_shape=(
            jax.ShapeDtypeStruct((slots, width), F32),
            jax.ShapeDtypeStruct((2, live_rows, kv_w), BF16),
        ),
        in_specs=[any_spec] + [vmem_spec] * 5 + [any_spec] * 4,
        out_specs=(vmem_spec, vmem_spec),
        scratch_shapes=[
            pltpu.VMEM((2, members, rows, width), BF16),
            pltpu.VMEM(qkv_weight.shape, BF16),
            pltpu.VMEM(fc_weight.shape, BF16),
            pltpu.VMEM((kv_w + ff, model), BF16),
            pltpu.VMEM((rows, model), BF16),
            pltpu.VMEM((rows, model), BF16),
            pltpu.VMEM((4, members, width), F32),
            pltpu.VMEM((slots, 128), F32),
            pltpu.VMEM((3, slots, 128), F32),
            pltpu.VMEM((rows, kv_w), BF16),
            pltpu.VMEM((slots, 2 * kv_w), BF16),
            pltpu.VMEM((rows, kv_w + ff), BF16),
            pltpu.VMEM((slots, 2 * kv_w), BF16),
            pltpu.VMEM((slots, 2 * kv_w), BF16),
            pltpu.VMEM((8, 128), F32),
            pltpu.VMEM((groups, 8, 128), F32),
            pltpu.VMEM((2, chips, rows, width), BF16),
            pltpu.VMEM((2, chips, rows, width), BF16),
            pltpu.VMEM((2, chips, rows, width), F32),
            pltpu.VMEM((2, 2, half, width), BF16),
            pltpu.VMEM((2, 2, half, width), BF16),
            pltpu.VMEM((2, 2, 2, half, width), BF16),
            pltpu.VMEM((2, 2, 2, half, width), BF16),
            dma((4,)),
            dma((2,)),
            dma((2, 11)),
            dma((2, 11)),
            dma((groups,)),
            dma((groups,)),
            dma((groups,)),
            dma((groups,)),
            dma((2, chips)),
            dma((2, chips)),
            dma((2, 2)),
            dma((2, 2)),
            dma((2, 2, 2)),
            dma((2, 2, 2)),
        ],
        compiler_params=pltpu.CompilerParams(
            collective_id=0, has_side_effects=True, vmem_limit_bytes=62 * 1024 * 1024
        ),
    )(
        activations,
        slot_segment.reshape(slots // 128, 128),
        *vecs,
        qkv_weight,
        dense_weight,
        fc_weight,
        proj_weight,
    )


def solution(mesh):
    placed = (
        P("req", "mlp"),
        P("req"),
        P(),
        P(),
        P(),
        P(),
        P(None, "mlp"),
        P("mlp", None),
        P(None, "mlp"),
        P("mlp", None),
    )
    return jax.shard_map(
        body,
        mesh=mesh,
        in_specs=placed,
        out_specs=(P("req", "mlp"), P(None, "req", "mlp")),
        check_vma=False,
    )
```

```python
import functools
import math

import jax
import jax.numpy as jnp
from jax import lax
from jax.experimental import pallas as pl
from jax.experimental.pallas import tpu as pltpu
from jax.sharding import PartitionSpec as P

HD = 128
ROT = 32
F32 = jnp.float32
BF16 = jnp.bfloat16
MESH = pl.DeviceIdType.MESH

LA, LB, OA, RA, RB, OB, PP, PL, PR, POA, POB = range(11)
OWN, RIGHT, OPP, LEFT = 0, 1, 2, 3
PIECES = ((0, 128), (128, 256), (384, 128))


def remote(src, dst, send_sem, recv_sem, dev):
    return pltpu.make_async_remote_copy(
        src_ref=src,
        dst_ref=dst,
        send_sem=send_sem,
        recv_sem=recv_sem,
        device_id=dev,
        device_id_type=MESH,
    )


def layer_kernel(
    groups,
    members,
    act,
    seg,
    g1,
    b1,
    g2,
    b2,
    wq_h,
    wd_h,
    wf_h,
    wp_h,
    out,
    cache,
    xf,
    wq,
    wf,
    wo,
    n1,
    n2,
    gs,
    segc,
    tab,
    qb,
    kvb,
    hc,
    kvp,
    kvr,
    cnt_s,
    cnt_r,
    psend,
    precv,
    mine,
    lo_s,
    lo_r,
    lb_s,
    lb_r,
    stat,
    outv,
    cachev,
    osem,
    wsem,
    lsem,
    ag_ss,
    ag_rs,
    kv_ss,
    kv_rs,
    ct_ss,
    ct_rs,
    p_ss,
    p_rs,
    lo_ss,
    lo_rs,
    lb_ss,
    lb_rs,
):
    width = xf.shape[2]
    chips = members // 2
    model = members * width
    heads = qb.shape[1] // HD
    kv_w = heads * HD
    per_peer = kvp.shape[0] // groups
    me_g = lax.axis_index("req")
    me = lax.axis_index("mlp")
    core = lax.rem(me, 2)
    chip = me // 2
    right = lax.rem(me + 2, members)
    left = lax.rem(me + members - 2, members)
    opp = lax.rem(me + members // 2, members)
    flip = 1 - 2 * core
    partner = me + flip
    to_right, to_left, to_partner = (me_g, right), (me_g, left), (me_g, partner)

    copies = [
        pltpu.make_async_copy(wq_h, wq, wsem.at[0]),
        pltpu.make_async_copy(wf_h, wf, wsem.at[1]),
        pltpu.make_async_copy(wd_h, wo.at[pl.ds(0, kv_w)], wsem.at[2]),
        pltpu.make_async_copy(wp_h, wo.at[pl.ds(kv_w, wo.shape[0] - kv_w)], wsem.at[3]),
    ]
    own_copies = [
        pltpu.make_async_copy(act.at[pl.ds(base, rows)], xf.at[me, pl.ds(base, rows)], lsem.at[h])
        for h, (base, rows) in enumerate(PIECES)
    ]

    barrier = pltpu.get_barrier_semaphore()
    for dev in (to_right, to_left, to_partner):
        pl.semaphore_signal(barrier, inc=1, device_id=dev, device_id_type=MESH)

    def greet(t, carry):
        peer = lax.rem(me_g + t, groups)
        pl.semaphore_signal(barrier, inc=1, device_id=(peer, me), device_id_type=MESH)
        return carry

    lax.fori_loop(1, groups, greet, 0)
    for c in own_copies + copies:
        c.start()
    pl.semaphore_wait(barrier, 3 + groups - 1)

    def span(h):
        base, rows = PIECES[h]
        return pl.ds(base, rows)

    def upper(h):
        base, rows = PIECES[h]
        return pl.ds(base, rows // 2)

    def lower(h):
        base, rows = PIECES[h]
        return pl.ds(base + rows // 2, rows // 2)

    def ag(h, kind, src, dst, dev):
        return remote(src, dst, ag_ss.at[h, kind], ag_rs.at[h, kind], dev)

    def got(h, kind, ref):
        remote(ref, ref, ag_ss.at[h, kind], ag_rs.at[h, kind], to_partner).wait_recv()

    sent = []

    def go(copy):
        copy.start()
        sent.append(copy)

    def gather_own(h):
        a = act.at[upper(h)]
        b = act.at[lower(h)]
        go(ag(h, LA, a, xf.at[me, upper(h)], to_right))
        go(ag(h, RB, b, xf.at[me, lower(h)], to_left))
        go(ag(h, LB, b, xf.at[me, lower(h)], to_right))
        go(ag(h, RA, a, xf.at[me, upper(h)], to_left))
        go(ag(h, PP, act.at[span(h)], xf.at[me, span(h)], to_partner))

    def gather_far(h):
        got(h, LA, xf.at[left, upper(h)])
        go(ag(h, OA, xf.at[left, upper(h)], xf.at[left, upper(h)], to_right))
        got(h, RB, xf.at[right, lower(h)])
        go(ag(h, OB, xf.at[right, lower(h)], xf.at[right, lower(h)], to_left))

    def gather_near(h):
        got(h, LB, xf.at[left, lower(h)])
        go(ag(h, PL, xf.at[left, span(h)], xf.at[left, span(h)], to_partner))
        got(h, RA, xf.at[right, upper(h)])
        go(ag(h, PR, xf.at[right, span(h)], xf.at[right, span(h)], to_partner))

    def gather_opp(h):
        got(h, OA, xf.at[opp, upper(h)])
        go(ag(h, POA, xf.at[opp, upper(h)], xf.at[opp, upper(h)], to_partner))
        got(h, OB, xf.at[opp, lower(h)])
        go(ag(h, POB, xf.at[opp, lower(h)], xf.at[opp, lower(h)], to_partner))

    def gather_end(h):
        own_copies[h].wait()
        got(h, PP, xf.at[partner, span(h)])
        got(h, PL, xf.at[left + flip, span(h)])
        got(h, PR, xf.at[right + flip, span(h)])
        got(h, POA, xf.at[opp + flip, upper(h)])
        got(h, POB, xf.at[opp + flip, lower(h)])

    gather_own(0)

    for i, ref in enumerate((g1, b1, g2, b2)):
        for m in range(members):
            for t in range(width // 128):
                k = m * (width // 128) + t
                gs[i, m : m + 1, t * 128 : (t + 1) * 128] = ref[k : k + 1, :]
    live_sum = jnp.sum((seg[...] >= 0).astype(F32), axis=1, keepdims=True)
    units = jnp.sum(live_sum, axis=0, keepdims=True) * (1.0 / groups)
    cnt_s[...] = jnp.broadcast_to(units, cnt_s.shape)
    for b in range(seg.shape[0]):
        block = jnp.broadcast_to(seg[b : b + 1, :].astype(F32), (128, 128))
        segc[b * 128 : (b + 1) * 128, :] = block.T

    lane = lax.broadcasted_iota(jnp.int32, (128, 128), 1)
    pair = lax.rem(lane, ROT // 2).astype(F32)
    freq = jnp.where(lane < ROT, jnp.exp(pair * (-2.0 / ROT * math.log(10000.0))), 0.0)

    def angles(b, carry):
        at = pl.ds(pl.multiple_of(b * 128, 128), 128)
        slot = (b * 128 + lax.broadcasted_iota(jnp.int32, (128, 128), 0)).astype(F32)
        ang = (slot - segc[at, :]) * freq
        sine = jnp.sin(ang)
        tab[0, at, :] = jnp.cos(ang)
        tab[1, at, :] = jnp.where(lane < ROT // 2, -sine, 0.0)
        tab[2, at, :] = jnp.where(lane < ROT // 2, 0.0, sine)
        return carry

    gather_far(0)
    gather_own(1)
    lax.fori_loop(0, seg.shape[0], angles, 0)
    gather_near(0)
    gather_opp(0)

    def count_out(t, carry):
        peer = lax.rem(me_g + t, groups)
        remote(cnt_s, cnt_r.at[me_g], ct_ss.at[t], ct_rs.at[t], (peer, me)).start()
        return carry

    lax.fori_loop(1, groups, count_out, 0)

    def norms(h):
        base, rows = PIECES[h]
        tiles = [(m, slice(k * 128, (k + 1) * 128)) for m in range(members) for k in range(width // 128)]

        def sums(r, carry):
            to = pl.ds(pl.multiple_of(r * 16, 16), 16)
            at = pl.ds(pl.multiple_of(base + r * 16, 16), 16)
            parts = [jnp.zeros((16, 128), F32)] * 4
            for n, (m, cols) in enumerate(tiles):
                parts[n % 4] = parts[n % 4] + xf[m, at, cols].astype(F32)
            stat[2, to, :] = (parts[0] + parts[1]) + (parts[2] + parts[3])
            return carry

        def squares(r, carry):
            to = pl.ds(pl.multiple_of(r * 16, 16), 16)
            at = pl.ds(pl.multiple_of(base + r * 16, 16), 16)
            mean = stat[0, to, :]
            parts = [jnp.zeros((16, 128), F32)] * 4
            for n, (m, cols) in enumerate(tiles):
                c = xf[m, at, cols].astype(F32) - mean
                parts[n % 4] = parts[n % 4] + c * c
            stat[2, to, :] = (parts[0] + parts[1]) + (parts[2] + parts[3])
            return carry

        def apply(r, carry):
            to = pl.ds(pl.multiple_of(r * 32, 32), 32)
            at = pl.ds(pl.multiple_of(base + r * 32, 32), 32)
            mean, scale = stat[0, to, :], stat[1, to, :]
            for m, cols in tiles:
                y = (xf[m, at, cols].astype(F32) - mean) * scale
                k = slice(m * width + cols.start, m * width + cols.stop)
                n1[to, k] = (y * gs[0, m : m + 1, cols] + gs[1, m : m + 1, cols]).astype(BF16)
                n2[to, k] = (y * gs[2, m : m + 1, cols] + gs[3, m : m + 1, cols]).astype(BF16)
            return carry

        lax.fori_loop(0, rows // 16, sums, 0)
        mean = jnp.sum(stat[2, 0:rows, :], axis=-1, keepdims=True) * (1.0 / model)
        stat[0, 0:rows, :] = jnp.broadcast_to(mean, (rows, 128))
        lax.fori_loop(0, rows // 16, squares, 0)
        var = jnp.sum(stat[2, 0:rows, :], axis=-1, keepdims=True) * (1.0 / model)
        stat[1, 0:rows, :] = jnp.broadcast_to(lax.rsqrt(var + 1e-05), (rows, 128))
        lax.fori_loop(0, rows // 32, apply, 0)

    def project(h):
        base, rows = PIECES[h]
        at = slice(base, base + rows)
        parts = []
        for n in range(wq.shape[1] // 256):
            acc = jnp.dot(n1[0:rows, :], wq[:, n * 256 : (n + 1) * 256], preferred_element_type=F32)
            parts += [acc[:, :HD], acc[:, HD:]]
        cos, s1, s2 = tab[0, at, :], tab[1, at, :], tab[2, at, :]

        def turn(u):
            return u * cos + pltpu.roll(u, HD - ROT // 2, 1) * s1 + pltpu.roll(u, ROT // 2, 1) * s2

        for i in range(heads):
            cols = slice(i * HD, (i + 1) * HD)
            qb[0:rows, cols] = turn(parts[3 * i]).astype(BF16)
            kvb[at, cols] = turn(parts[3 * i + 1]).astype(BF16)
            kvb[at, kv_w + i * HD : kv_w + (i + 1) * HD] = parts[3 * i + 2].astype(BF16)

    def attend(h):
        base, rows = PIECES[h]
        keys = base + rows
        first = jnp.concatenate([segc[base : base + rows, :]] * (keys // 128), axis=1)
        query = (base + lax.broadcasted_iota(jnp.int32, (rows, keys), 0)).astype(F32)
        key = lax.broadcasted_iota(jnp.int32, (rows, keys), 1).astype(F32)
        allowed = (key >= first) & (key <= query)
        for i in range(heads):
            cols = slice(i * HD, (i + 1) * HD)
            s = lax.dot_general(
                qb[0:rows, cols],
                kvb[0:keys, cols],
                (((1,), (1,)), ((), ())),
                preferred_element_type=F32,
            ) * (HD**-0.5)
            s = jnp.where(allowed, s, -1e30)
            w = jnp.exp(s - jnp.max(s, axis=-1, keepdims=True))
            p = (w / jnp.sum(w, axis=-1, keepdims=True)).astype(BF16)
            ctx = jnp.dot(
                p, kvb[0:keys, kv_w + i * HD : kv_w + (i + 1) * HD], preferred_element_type=F32
            )
            hc[0:rows, cols] = ctx.astype(BF16)

    def expand(h):
        rows = PIECES[h][1]
        for n in range(wf.shape[1] // 256):
            cols = slice(n * 256, (n + 1) * 256)
            u = jnp.dot(n2[0:rows, :], wf[:, cols], preferred_element_type=F32)
            u = 0.5 * u * (1.0 + lax.erf(u * (0.5**0.5)))
            hc[0:rows, kv_w + n * 256 : kv_w + (n + 1) * 256] = u.astype(BF16)

    def pcopy(h, rel):
        return remote(psend.at[rel, span(h)], precv.at[rel, span(h)], p_ss.at[h, rel], p_rs.at[h, rel], to_partner)

    def contract(h, rel):
        base, rows = PIECES[h]
        block = 2 * lax.rem(chip + rel, chips)
        for theirs in (True, False):
            col = (block + (1 - core if theirs else core)) * width
            acc = jnp.dot(
                hc[0:rows, :],
                wo[:, pl.ds(pl.multiple_of(col, width), width)],
                preferred_element_type=F32,
            )
            if theirs:
                psend[rel, base : base + rows, :] = acc.astype(BF16)
                go(pcopy(h, rel))
            else:
                mine[rel, base : base + rows, :] = acc

    def side(h, piece):
        base, rows = PIECES[h]
        half = rows // 2
        return slice(base + piece * half, base + (piece + 1) * half)

    def fold(h):
        base, rows = PIECES[h]
        return pl.ds(base // 2, rows // 2)

    def chip_sum(h, rel, piece):
        at = side(h, piece)
        return mine[rel, at, :] + precv[rel, at, :].astype(F32)

    def low(h, way):
        dev = to_right if way == 0 else to_left
        return remote(lo_s.at[way, fold(h)], lo_r.at[way, fold(h)], lo_ss.at[h, way], lo_rs.at[h, way], dev)

    def back(h, way, piece):
        dev = to_right if way == 0 else to_left
        return remote(
            lb_s.at[way, piece, fold(h)],
            lb_r.at[way, piece, fold(h)],
            lb_ss.at[h, way, piece],
            lb_rs.at[h, way, piece],
            dev,
        )

    def scatter_opp(h):
        pcopy(h, OPP).wait_recv()
        lo_s[0, fold(h)] = chip_sum(h, OPP, 0).astype(BF16)
        go(low(h, 0))
        lo_s[1, fold(h)] = chip_sum(h, OPP, 1).astype(BF16)
        go(low(h, 1))

    def scatter_near(h, way):
        rel = RIGHT if way == 0 else LEFT
        piece = 1 - way
        pcopy(h, rel).wait_recv()
        lb_s[way, piece, fold(h)] = chip_sum(h, rel, piece).astype(BF16)
        go(back(h, way, piece))

    def scatter_far(h):
        for way in range(2):
            rel = RIGHT if way == 0 else LEFT
            piece = way
            low(h, way).wait_recv()
            total = chip_sum(h, rel, piece) + lo_r[way, fold(h)].astype(F32)
            lb_s[way, piece, fold(h)] = total.astype(BF16)
            go(back(h, way, piece))

    def finish(h):
        pcopy(h, OWN).wait_recv()
        for piece in range(2):
            for way in range(2):
                back(h, way, piece).wait_recv()
            at = side(h, piece)
            total = chip_sum(h, OWN, piece)
            total = total + lb_r[0, piece, fold(h)].astype(F32) + lb_r[1, piece, fold(h)].astype(F32)
            x = xf[me, at, :].astype(F32)
            first = jnp.concatenate([segc[at, :]] * (width // 128), axis=1)
            outv[at, :] = jnp.where(first >= 0.0, x + total, 0.0)
        out_copy(h).start()

    def out_copy(h):
        return pltpu.make_async_copy(outv.at[span(h)], out.at[span(h)], osem.at[h])

    def cache_out():
        slots = kvp.shape[0]
        r = lax.broadcasted_iota(jnp.int32, (slots, slots), 0)
        s = lax.broadcasted_iota(jnp.int32, (slots, slots), 1)
        pick = s == lax.rem(r, per_peer) * groups + r // per_peer
        pick = jnp.where(pick, 1.0, 0.0).astype(BF16)
        kvp[...] = jnp.dot(pick, kvb[...], preferred_element_type=F32).astype(BF16)

        def body(t, carry):
            peer = lax.rem(me_g + t, groups)
            kv_copy(t, peer).start()
            return carry

        lax.fori_loop(1, groups, body, 0)

    def kv_copy(t, peer):
        src = kvp.at[pl.ds(pl.multiple_of(peer * per_peer, per_peer), per_peer)]
        dst = kvr.at[pl.ds(pl.multiple_of(me_g * per_peer, per_peer), per_peer)]
        return remote(src, dst, kv_ss.at[t], kv_rs.at[t], (peer, me))

    def cache_in():
        here = pl.ds(pl.multiple_of(me_g * per_peer, per_peer), per_peer)
        kvr[here, :] = kvp[here, :]
        cnt_r[me_g] = cnt_s[...]

        def body(t, carry):
            peer = lax.rem(me_g + groups - t, groups)
            from_peer = pl.ds(pl.multiple_of(peer * per_peer, per_peer), per_peer)
            dst = kvr.at[from_peer]
            remote(dst, dst, kv_ss.at[t], kv_rs.at[t], (peer, me)).wait_recv()
            dst = cnt_r.at[peer]
            remote(dst, dst, ct_ss.at[t], ct_rs.at[t], (peer, me)).wait_recv()
            return carry

        lax.fori_loop(1, groups, body, 0)
        per_block = 128 // per_peer
        live_rows = cache.shape[1]
        row = lax.broadcasted_iota(jnp.int32, (live_rows, 128), 0).astype(F32)
        lane1 = lax.broadcasted_iota(jnp.int32, (1, 128), 1)
        owner = lane1 // per_peer
        unit = lax.rem(lane1, per_peer).astype(F32)
        before = jnp.zeros((1, 128), F32)
        acc = jnp.zeros((live_rows, kvr.shape[1]), F32)
        for b in range(groups // per_block):
            have = jnp.zeros((1, 128), F32)
            start = jnp.zeros((1, 128), F32)
            for t in range(per_block):
                count = cnt_r[b * per_block + t, 0:1, :]
                have = jnp.where(owner == t, count, have)
                start = jnp.where(owner == t, before, start)
                before = before + count
            place = jnp.where(unit < have, start + unit, -1.0)
            pick = jnp.where(row == place, 1.0, 0.0).astype(BF16)
            acc = acc + jnp.dot(
                pick, kvr[b * 128 : (b + 1) * 128, :], preferred_element_type=F32
            )
        cachev[0] = acc[:, :kv_w].astype(BF16)
        cachev[1] = acc[:, kv_w:].astype(BF16)
        cache_copy.start()

    cache_copy = pltpu.make_async_copy(cachev, cache, osem.at[len(PIECES)])

    gather_end(0)
    norms(0)
    copies[0].wait()
    project(0)
    gather_far(1)
    gather_own(2)
    attend(0)
    copies[1].wait()
    expand(0)
    gather_near(1)
    copies[2].wait()
    copies[3].wait()
    contract(0, OPP)
    contract(0, RIGHT)
    scatter_opp(0)
    contract(0, LEFT)
    gather_opp(1)
    scatter_near(0, 0)
    contract(0, OWN)
    scatter_near(0, 1)
    gather_far(2)
    gather_end(1)
    norms(1)
    gather_near(2)
    scatter_far(0)
    project(1)
    gather_opp(2)
    attend(1)
    expand(1)
    contract(1, OPP)
    contract(1, RIGHT)
    scatter_opp(1)
    contract(1, LEFT)
    scatter_near(1, 0)
    contract(1, OWN)
    scatter_near(1, 1)
    gather_end(2)
    norms(2)
    project(2)
    cache_out()
    attend(2)
    scatter_far(1)
    expand(2)
    contract(2, OPP)
    contract(2, RIGHT)
    scatter_opp(2)
    contract(2, LEFT)
    scatter_near(2, 0)
    contract(2, OWN)
    scatter_near(2, 1)
    finish(0)
    scatter_far(2)
    cache_in()
    finish(1)
    finish(2)

    for copy in sent:
        copy.wait_send()

    def drain(t, carry):
        peer = lax.rem(me_g + t, groups)
        kv_copy(t, peer).wait_send()
        remote(cnt_s, cnt_r.at[me_g], ct_ss.at[t], ct_rs.at[t], (peer, me)).wait_send()
        return carry

    lax.fori_loop(1, groups, drain, 0)
    cache_copy.wait()
    for h in range(len(PIECES)):
        out_copy(h).wait()


def body(
    activations,
    slot_segment,
    attn_norm_gain,
    attn_norm_bias,
    mlp_norm_gain,
    mlp_norm_bias,
    qkv_weight,
    dense_weight,
    fc_weight,
    proj_weight,
):
    slots, width = activations.shape
    groups = lax.axis_size("req")
    members = lax.axis_size("mlp")
    model = qkv_weight.shape[0]
    pieces = len(PIECES)
    rows = max(size for _, size in PIECES)
    half = slots // 2
    kv_w = dense_weight.shape[0]
    ff = fc_weight.shape[1]
    live_rows = slots // 2
    chips = members // 2
    dma = pltpu.SemaphoreType.DMA
    any_spec = pl.BlockSpec(memory_space=pl.ANY)
    vmem_spec = pl.BlockSpec(memory_space=pltpu.VMEM)
    vecs = [
        v.reshape(model // 128, 128)
        for v in (attn_norm_gain, attn_norm_bias, mlp_norm_gain, mlp_norm_bias)
    ]
    return pl.pallas_call(
        functools.partial(layer_kernel, groups, members),
        name="layer",
        out_shape=(
            jax.ShapeDtypeStruct((slots, width), F32),
            jax.ShapeDtypeStruct((2, live_rows, kv_w), BF16),
        ),
        in_specs=[any_spec] + [vmem_spec] * 5 + [any_spec] * 4,
        out_specs=(any_spec, any_spec),
        scratch_shapes=[
            pltpu.VMEM((members, slots, width), BF16),
            pltpu.VMEM(qkv_weight.shape, BF16),
            pltpu.VMEM(fc_weight.shape, BF16),
            pltpu.VMEM((kv_w + ff, model), BF16),
            pltpu.VMEM((rows, model), BF16),
            pltpu.VMEM((rows, model), BF16),
            pltpu.VMEM((4, members, width), F32),
            pltpu.VMEM((slots, 128), F32),
            pltpu.VMEM((3, slots, 128), F32),
            pltpu.VMEM((rows, kv_w), BF16),
            pltpu.VMEM((slots, 2 * kv_w), BF16),
            pltpu.VMEM((rows, kv_w + ff), BF16),
            pltpu.VMEM((slots, 2 * kv_w), BF16),
            pltpu.VMEM((slots, 2 * kv_w), BF16),
            pltpu.VMEM((8, 128), F32),
            pltpu.VMEM((groups, 8, 128), F32),
            pltpu.VMEM((chips, slots, width), BF16),
            pltpu.VMEM((chips, slots, width), BF16),
            pltpu.VMEM((chips, slots, width), F32),
            pltpu.VMEM((2, half, width), BF16),
            pltpu.VMEM((2, half, width), BF16),
            pltpu.VMEM((2, 2, half, width), BF16),
            pltpu.VMEM((2, 2, half, width), BF16),
            pltpu.VMEM((3, rows, 128), F32),
            pltpu.VMEM((slots, width), F32),
            pltpu.VMEM((2, live_rows, kv_w), BF16),
            dma((pieces + 1,)),
            dma((4,)),
            dma((pieces,)),
            dma((pieces, 11)),
            dma((pieces, 11)),
            dma((groups,)),
            dma((groups,)),
            dma((groups,)),
            dma((groups,)),
            dma((pieces, chips)),
            dma((pieces, chips)),
            dma((pieces, 2)),
            dma((pieces, 2)),
            dma((pieces, 2, 2)),
            dma((pieces, 2, 2)),
        ],
        compiler_params=pltpu.CompilerParams(
            collective_id=0, has_side_effects=True, vmem_limit_bytes=62 * 1024 * 1024
        ),
    )(
        activations,
        slot_segment.reshape(slots // 128, 128),
        *vecs,
        qkv_weight,
        dense_weight,
        fc_weight,
        proj_weight,
    )


def solution(mesh):
    placed = (
        P("req", "mlp"),
        P("req"),
        P(),
        P(),
        P(),
        P(),
        P(None, "mlp"),
        P("mlp", None),
        P(None, "mlp"),
        P("mlp", None),
    )
    return jax.shard_map(
        body,
        mesh=mesh,
        in_specs=placed,
        out_specs=(P("req", "mlp"), P(None, "req", "mlp")),
        check_vma=False,
    )
```

```python
import functools
import math

import jax
import jax.numpy as jnp
from jax import lax
from jax.experimental import pallas as pl
from jax.experimental.pallas import tpu as pltpu
from jax.sharding import PartitionSpec as P

HD = 128
ROT = 32
F32 = jnp.float32
BF16 = jnp.bfloat16
MESH = pl.DeviceIdType.MESH

LA, LB, OA, RA, RB, OB, PP, PL, PR, POA, POB = range(11)
OWN, RIGHT, OPP, LEFT = 0, 1, 2, 3
PIECES = ((0, 128), (128, 256), (384, 128))


def remote(src, dst, send_sem, recv_sem, dev):
    return pltpu.make_async_remote_copy(
        src_ref=src,
        dst_ref=dst,
        send_sem=send_sem,
        recv_sem=recv_sem,
        device_id=dev,
        device_id_type=MESH,
    )


def layer_kernel(
    groups,
    members,
    act,
    seg,
    g1,
    b1,
    g2,
    b2,
    wq_h,
    wd_h,
    wf_h,
    wp_h,
    out,
    cache,
    xf,
    wq,
    wf,
    wo,
    n1,
    n2,
    gs,
    segc,
    tab,
    qb,
    kvb,
    hc,
    kvp,
    kvr,
    cnt_s,
    cnt_r,
    psend,
    precv,
    mine,
    lo_s,
    lo_r,
    lb_s,
    lb_r,
    stat,
    outv,
    cachev,
    osem,
    wsem,
    lsem,
    ag_ss,
    ag_rs,
    kv_ss,
    kv_rs,
    ct_ss,
    ct_rs,
    p_ss,
    p_rs,
    lo_ss,
    lo_rs,
    lb_ss,
    lb_rs,
):
    width = xf.shape[2]
    chips = members // 2
    model = members * width
    heads = qb.shape[1] // HD
    kv_w = heads * HD
    per_peer = kvp.shape[0] // groups
    me_g = lax.axis_index("req")
    me = lax.axis_index("mlp")
    core = lax.rem(me, 2)
    chip = me // 2
    right = lax.rem(me + 2, members)
    left = lax.rem(me + members - 2, members)
    opp = lax.rem(me + members // 2, members)
    flip = 1 - 2 * core
    partner = me + flip
    to_right, to_left, to_partner = (me_g, right), (me_g, left), (me_g, partner)

    copies = [
        pltpu.make_async_copy(wq_h, wq, wsem.at[0]),
        pltpu.make_async_copy(wf_h, wf, wsem.at[1]),
        pltpu.make_async_copy(wd_h, wo.at[pl.ds(0, kv_w)], wsem.at[2]),
        pltpu.make_async_copy(wp_h, wo.at[pl.ds(kv_w, wo.shape[0] - kv_w)], wsem.at[3]),
    ]
    own_copies = [
        pltpu.make_async_copy(act.at[pl.ds(base, rows)], xf.at[me, pl.ds(base, rows)], lsem.at[h])
        for h, (base, rows) in enumerate(PIECES)
    ]

    barrier = pltpu.get_barrier_semaphore()
    for dev in (to_right, to_left, to_partner):
        pl.semaphore_signal(barrier, inc=1, device_id=dev, device_id_type=MESH)

    def greet(t, carry):
        peer = lax.rem(me_g + t, groups)
        pl.semaphore_signal(barrier, inc=1, device_id=(peer, me), device_id_type=MESH)
        return carry

    lax.fori_loop(1, groups, greet, 0)
    for c in own_copies + copies:
        c.start()
    pl.semaphore_wait(barrier, 3 + groups - 1)

    def span(h):
        base, rows = PIECES[h]
        return pl.ds(base, rows)

    def upper(h):
        base, rows = PIECES[h]
        return pl.ds(base, rows // 2)

    def lower(h):
        base, rows = PIECES[h]
        return pl.ds(base + rows // 2, rows // 2)

    def ag(h, kind, src, dst, dev):
        return remote(src, dst, ag_ss.at[h, kind], ag_rs.at[h, kind], dev)

    def got(h, kind, ref):
        remote(ref, ref, ag_ss.at[h, kind], ag_rs.at[h, kind], to_partner).wait_recv()

    sent = []

    def go(copy):
        copy.start()
        sent.append(copy)

    def gather_own(h):
        a = act.at[upper(h)]
        b = act.at[lower(h)]
        go(ag(h, LA, a, xf.at[me, upper(h)], to_right))
        go(ag(h, RB, b, xf.at[me, lower(h)], to_left))
        go(ag(h, LB, b, xf.at[me, lower(h)], to_right))
        go(ag(h, RA, a, xf.at[me, upper(h)], to_left))
        go(ag(h, PP, act.at[span(h)], xf.at[me, span(h)], to_partner))

    def gather_far(h):
        got(h, LA, xf.at[left, upper(h)])
        go(ag(h, OA, xf.at[left, upper(h)], xf.at[left, upper(h)], to_right))
        got(h, RB, xf.at[right, lower(h)])
        go(ag(h, OB, xf.at[right, lower(h)], xf.at[right, lower(h)], to_left))

    def gather_near(h):
        got(h, LB, xf.at[left, lower(h)])
        go(ag(h, PL, xf.at[left, span(h)], xf.at[left, span(h)], to_partner))
        got(h, RA, xf.at[right, upper(h)])
        go(ag(h, PR, xf.at[right, span(h)], xf.at[right, span(h)], to_partner))

    def gather_opp(h):
        got(h, OA, xf.at[opp, upper(h)])
        go(ag(h, POA, xf.at[opp, upper(h)], xf.at[opp, upper(h)], to_partner))
        got(h, OB, xf.at[opp, lower(h)])
        go(ag(h, POB, xf.at[opp, lower(h)], xf.at[opp, lower(h)], to_partner))

    def gather_end(h):
        own_copies[h].wait()
        got(h, PP, xf.at[partner, span(h)])
        got(h, PL, xf.at[left + flip, span(h)])
        got(h, PR, xf.at[right + flip, span(h)])
        got(h, POA, xf.at[opp + flip, upper(h)])
        got(h, POB, xf.at[opp + flip, lower(h)])

    gather_own(0)

    for i, ref in enumerate((g1, b1, g2, b2)):
        for m in range(members):
            for t in range(width // 128):
                k = m * (width // 128) + t
                gs[i, m : m + 1, t * 128 : (t + 1) * 128] = ref[k : k + 1, :]
    live_sum = jnp.sum((seg[...] >= 0).astype(F32), axis=1, keepdims=True)
    units = jnp.sum(live_sum, axis=0, keepdims=True) * (1.0 / groups)
    cnt_s[...] = jnp.broadcast_to(units, cnt_s.shape)
    for b in range(seg.shape[0]):
        block = jnp.broadcast_to(seg[b : b + 1, :].astype(F32), (128, 128))
        segc[b * 128 : (b + 1) * 128, :] = block.T

    lane = lax.broadcasted_iota(jnp.int32, (128, 128), 1)
    pair = lax.rem(lane, ROT // 2).astype(F32)
    freq = jnp.where(lane < ROT, jnp.exp(pair * (-2.0 / ROT * math.log(10000.0))), 0.0)

    def angles(b, carry):
        at = pl.ds(pl.multiple_of(b * 128, 128), 128)
        slot = (b * 128 + lax.broadcasted_iota(jnp.int32, (128, 128), 0)).astype(F32)
        ang = (slot - segc[at, :]) * freq
        sine = jnp.sin(ang)
        tab[0, at, :] = jnp.cos(ang)
        tab[1, at, :] = jnp.where(lane < ROT // 2, -sine, 0.0)
        tab[2, at, :] = jnp.where(lane < ROT // 2, 0.0, sine)
        return carry

    gather_far(0)
    gather_own(1)
    lax.fori_loop(0, seg.shape[0] // 2, angles, 0)
    gather_near(0)
    lax.fori_loop(seg.shape[0] // 2, seg.shape[0], angles, 0)
    gather_opp(0)

    def count_out(t, carry):
        peer = lax.rem(me_g + t, groups)
        remote(cnt_s, cnt_r.at[me_g], ct_ss.at[t], ct_rs.at[t], (peer, me)).start()
        return carry

    lax.fori_loop(1, groups, count_out, 0)

    def norms(h):
        base, rows = PIECES[h]
        tiles = [(m, slice(k * 128, (k + 1) * 128)) for m in range(members) for k in range(width // 128)]

        def sums(r, carry):
            to = pl.ds(pl.multiple_of(r * 16, 16), 16)
            at = pl.ds(pl.multiple_of(base + r * 16, 16), 16)
            parts = [jnp.zeros((16, 128), F32)] * 4
            for n, (m, cols) in enumerate(tiles):
                parts[n % 4] = parts[n % 4] + xf[m, at, cols].astype(F32)
            stat[2, to, :] = (parts[0] + parts[1]) + (parts[2] + parts[3])
            return carry

        def squares(r, carry):
            to = pl.ds(pl.multiple_of(r * 16, 16), 16)
            at = pl.ds(pl.multiple_of(base + r * 16, 16), 16)
            mean = stat[0, to, :]
            parts = [jnp.zeros((16, 128), F32)] * 4
            for n, (m, cols) in enumerate(tiles):
                c = xf[m, at, cols].astype(F32) - mean
                parts[n % 4] = parts[n % 4] + c * c
            stat[2, to, :] = (parts[0] + parts[1]) + (parts[2] + parts[3])
            return carry

        def apply(r, carry):
            to = pl.ds(pl.multiple_of(r * 32, 32), 32)
            at = pl.ds(pl.multiple_of(base + r * 32, 32), 32)
            mean, scale = stat[0, to, :], stat[1, to, :]
            for m, cols in tiles:
                y = (xf[m, at, cols].astype(F32) - mean) * scale
                k = slice(m * width + cols.start, m * width + cols.stop)
                n1[to, k] = (y * gs[0, m : m + 1, cols] + gs[1, m : m + 1, cols]).astype(BF16)
                n2[to, k] = (y * gs[2, m : m + 1, cols] + gs[3, m : m + 1, cols]).astype(BF16)
            return carry

        lax.fori_loop(0, rows // 16, sums, 0)
        mean = jnp.sum(stat[2, 0:rows, :], axis=-1, keepdims=True) * (1.0 / model)
        stat[0, 0:rows, :] = jnp.broadcast_to(mean, (rows, 128))
        lax.fori_loop(0, rows // 16, squares, 0)
        var = jnp.sum(stat[2, 0:rows, :], axis=-1, keepdims=True) * (1.0 / model)
        stat[1, 0:rows, :] = jnp.broadcast_to(lax.rsqrt(var + 1e-05), (rows, 128))
        lax.fori_loop(0, rows // 32, apply, 0)

    def project(h):
        base, rows = PIECES[h]
        at = slice(base, base + rows)
        parts = []
        for n in range(wq.shape[1] // 256):
            acc = jnp.dot(n1[0:rows, :], wq[:, n * 256 : (n + 1) * 256], preferred_element_type=F32)
            parts += [acc[:, :HD], acc[:, HD:]]
        cos, s1, s2 = tab[0, at, :], tab[1, at, :], tab[2, at, :]

        def turn(u):
            return u * cos + pltpu.roll(u, HD - ROT // 2, 1) * s1 + pltpu.roll(u, ROT // 2, 1) * s2

        for i in range(heads):
            cols = slice(i * HD, (i + 1) * HD)
            qb[0:rows, cols] = turn(parts[3 * i]).astype(BF16)
            kvb[at, cols] = turn(parts[3 * i + 1]).astype(BF16)
            kvb[at, kv_w + i * HD : kv_w + (i + 1) * HD] = parts[3 * i + 2].astype(BF16)

    def attend(h):
        base, rows = PIECES[h]
        keys = base + rows
        first = jnp.concatenate([segc[base : base + rows, :]] * (keys // 128), axis=1)
        query = (base + lax.broadcasted_iota(jnp.int32, (rows, keys), 0)).astype(F32)
        key = lax.broadcasted_iota(jnp.int32, (rows, keys), 1).astype(F32)
        allowed = (key >= first) & (key <= query)
        for i in range(heads):
            cols = slice(i * HD, (i + 1) * HD)
            s = lax.dot_general(
                qb[0:rows, cols],
                kvb[0:keys, cols],
                (((1,), (1,)), ((), ())),
                preferred_element_type=F32,
            ) * (HD**-0.5)
            s = jnp.where(allowed, s, -1e30)
            w = jnp.exp(s - jnp.max(s, axis=-1, keepdims=True))
            p = (w / jnp.sum(w, axis=-1, keepdims=True)).astype(BF16)
            ctx = jnp.dot(
                p, kvb[0:keys, kv_w + i * HD : kv_w + (i + 1) * HD], preferred_element_type=F32
            )
            hc[0:rows, cols] = ctx.astype(BF16)

    def expand(h):
        rows = PIECES[h][1]
        for n in range(wf.shape[1] // 256):
            cols = slice(n * 256, (n + 1) * 256)
            u = jnp.dot(n2[0:rows, :], wf[:, cols], preferred_element_type=F32)
            u = 0.5 * u * (1.0 + lax.erf(u * (0.5**0.5)))
            hc[0:rows, kv_w + n * 256 : kv_w + (n + 1) * 256] = u.astype(BF16)

    def pcopy(h, rel):
        return remote(psend.at[rel, span(h)], precv.at[rel, span(h)], p_ss.at[h, rel], p_rs.at[h, rel], to_partner)

    def contract(h, rel):
        base, rows = PIECES[h]
        block = 2 * lax.rem(chip + rel, chips)
        for theirs in (True, False):
            col = (block + (1 - core if theirs else core)) * width
            acc = jnp.dot(
                hc[0:rows, :],
                wo[:, pl.ds(pl.multiple_of(col, width), width)],
                preferred_element_type=F32,
            )
            if theirs:
                psend[rel, base : base + rows, :] = acc.astype(BF16)
                go(pcopy(h, rel))
            else:
                mine[rel, base : base + rows, :] = acc

    def side(h, piece):
        base, rows = PIECES[h]
        half = rows // 2
        return slice(base + piece * half, base + (piece + 1) * half)

    def fold(h):
        base, rows = PIECES[h]
        return pl.ds(base // 2, rows // 2)

    def chip_sum(h, rel, piece):
        at = side(h, piece)
        return mine[rel, at, :] + precv[rel, at, :].astype(F32)

    def low(h, way):
        dev = to_right if way == 0 else to_left
        return remote(lo_s.at[way, fold(h)], lo_r.at[way, fold(h)], lo_ss.at[h, way], lo_rs.at[h, way], dev)

    def back(h, way, piece):
        dev = to_right if way == 0 else to_left
        return remote(
            lb_s.at[way, piece, fold(h)],
            lb_r.at[way, piece, fold(h)],
            lb_ss.at[h, way, piece],
            lb_rs.at[h, way, piece],
            dev,
        )

    def scatter_opp(h):
        pcopy(h, OPP).wait_recv()
        lo_s[0, fold(h)] = chip_sum(h, OPP, 0).astype(BF16)
        go(low(h, 0))
        lo_s[1, fold(h)] = chip_sum(h, OPP, 1).astype(BF16)
        go(low(h, 1))

    def scatter_near(h, way):
        rel = RIGHT if way == 0 else LEFT
        piece = 1 - way
        pcopy(h, rel).wait_recv()
        lb_s[way, piece, fold(h)] = chip_sum(h, rel, piece).astype(BF16)
        go(back(h, way, piece))

    def scatter_far(h):
        for way in range(2):
            rel = RIGHT if way == 0 else LEFT
            piece = way
            low(h, way).wait_recv()
            total = chip_sum(h, rel, piece) + lo_r[way, fold(h)].astype(F32)
            lb_s[way, piece, fold(h)] = total.astype(BF16)
            go(back(h, way, piece))

    def finish(h):
        pcopy(h, OWN).wait_recv()
        for piece in range(2):
            for way in range(2):
                back(h, way, piece).wait_recv()
            at = side(h, piece)
            total = chip_sum(h, OWN, piece)
            total = total + lb_r[0, piece, fold(h)].astype(F32) + lb_r[1, piece, fold(h)].astype(F32)
            x = xf[me, at, :].astype(F32)
            first = jnp.concatenate([segc[at, :]] * (width // 128), axis=1)
            outv[at, :] = jnp.where(first >= 0.0, x + total, 0.0)
        out_copy(h).start()

    def out_copy(h):
        return pltpu.make_async_copy(outv.at[span(h)], out.at[span(h)], osem.at[h])

    def cache_out():
        slots = kvp.shape[0]
        r = lax.broadcasted_iota(jnp.int32, (slots, slots), 0)
        s = lax.broadcasted_iota(jnp.int32, (slots, slots), 1)
        pick = s == lax.rem(r, per_peer) * groups + r // per_peer
        pick = jnp.where(pick, 1.0, 0.0).astype(BF16)
        kvp[...] = jnp.dot(pick, kvb[...], preferred_element_type=F32).astype(BF16)

        def body(t, carry):
            peer = lax.rem(me_g + t, groups)
            kv_copy(t, peer).start()
            return carry

        lax.fori_loop(1, groups, body, 0)

    def kv_copy(t, peer):
        src = kvp.at[pl.ds(pl.multiple_of(peer * per_peer, per_peer), per_peer)]
        dst = kvr.at[pl.ds(pl.multiple_of(me_g * per_peer, per_peer), per_peer)]
        return remote(src, dst, kv_ss.at[t], kv_rs.at[t], (peer, me))

    def cache_in():
        here = pl.ds(pl.multiple_of(me_g * per_peer, per_peer), per_peer)
        kvr[here, :] = kvp[here, :]
        cnt_r[me_g] = cnt_s[...]

        def body(t, carry):
            peer = lax.rem(me_g + groups - t, groups)
            from_peer = pl.ds(pl.multiple_of(peer * per_peer, per_peer), per_peer)
            dst = kvr.at[from_peer]
            remote(dst, dst, kv_ss.at[t], kv_rs.at[t], (peer, me)).wait_recv()
            dst = cnt_r.at[peer]
            remote(dst, dst, ct_ss.at[t], ct_rs.at[t], (peer, me)).wait_recv()
            return carry

        lax.fori_loop(1, groups, body, 0)
        per_block = 128 // per_peer
        live_rows = cache.shape[1]
        row = lax.broadcasted_iota(jnp.int32, (live_rows, 128), 0).astype(F32)
        lane1 = lax.broadcasted_iota(jnp.int32, (1, 128), 1)
        owner = lane1 // per_peer
        unit = lax.rem(lane1, per_peer).astype(F32)
        before = jnp.zeros((1, 128), F32)
        acc = jnp.zeros((live_rows, kvr.shape[1]), F32)
        for b in range(groups // per_block):
            have = jnp.zeros((1, 128), F32)
            start = jnp.zeros((1, 128), F32)
            for t in range(per_block):
                count = cnt_r[b * per_block + t, 0:1, :]
                have = jnp.where(owner == t, count, have)
                start = jnp.where(owner == t, before, start)
                before = before + count
            place = jnp.where(unit < have, start + unit, -1.0)
            pick = jnp.where(row == place, 1.0, 0.0).astype(BF16)
            acc = acc + jnp.dot(
                pick, kvr[b * 128 : (b + 1) * 128, :], preferred_element_type=F32
            )
        cachev[0] = acc[:, :kv_w].astype(BF16)
        cachev[1] = acc[:, kv_w:].astype(BF16)
        cache_copy.start()

    cache_copy = pltpu.make_async_copy(cachev, cache, osem.at[len(PIECES)])

    gather_end(0)
    norms(0)
    copies[0].wait()
    project(0)
    gather_far(1)
    gather_own(2)
    attend(0)
    copies[1].wait()
    expand(0)
    gather_near(1)
    copies[2].wait()
    copies[3].wait()
    contract(0, OPP)
    contract(0, RIGHT)
    scatter_opp(0)
    contract(0, LEFT)
    gather_opp(1)
    scatter_near(0, 0)
    contract(0, OWN)
    scatter_near(0, 1)
    gather_far(2)
    gather_end(1)
    norms(1)
    gather_near(2)
    scatter_far(0)
    project(1)
    gather_opp(2)
    attend(1)
    expand(1)
    contract(1, OPP)
    contract(1, RIGHT)
    scatter_opp(1)
    contract(1, LEFT)
    scatter_near(1, 0)
    contract(1, OWN)
    scatter_near(1, 1)
    gather_end(2)
    norms(2)
    project(2)
    cache_out()
    attend(2)
    scatter_far(1)
    expand(2)
    contract(2, OPP)
    contract(2, RIGHT)
    scatter_opp(2)
    contract(2, LEFT)
    scatter_near(2, 0)
    contract(2, OWN)
    scatter_near(2, 1)
    finish(0)
    scatter_far(2)
    cache_in()
    finish(1)
    finish(2)

    for copy in sent:
        copy.wait_send()

    def drain(t, carry):
        peer = lax.rem(me_g + t, groups)
        kv_copy(t, peer).wait_send()
        remote(cnt_s, cnt_r.at[me_g], ct_ss.at[t], ct_rs.at[t], (peer, me)).wait_send()
        return carry

    lax.fori_loop(1, groups, drain, 0)
    cache_copy.wait()
    for h in range(len(PIECES)):
        out_copy(h).wait()


def deliver_kernel(rows_h, cache_h, rows_o, cache_o, rows_v, cache_v, isem, osem):
    step = rows_h.shape[0] // 4
    parts = [
        (rows_h.at[s], rows_v.at[s], rows_o.at[s])
        for s in (pl.ds(i * step, step) for i in range(4))
    ]
    parts.insert(0, (cache_h, cache_v, cache_o))
    inward = [pltpu.make_async_copy(a, v, isem.at[i]) for i, (a, v, _) in enumerate(parts)]
    outward = [pltpu.make_async_copy(v, o, osem.at[i]) for i, (_, v, o) in enumerate(parts)]
    for c in inward:
        c.start()
    for i, o in zip(inward, outward):
        i.wait()
        o.start()
    for o in outward:
        o.wait()


def deliver(rows, cache):
    any_spec = pl.BlockSpec(memory_space=pl.ANY)
    return pl.pallas_call(
        deliver_kernel,
        name="deliver",
        out_shape=(
            jax.ShapeDtypeStruct(rows.shape, rows.dtype),
            jax.ShapeDtypeStruct(cache.shape, cache.dtype),
        ),
        in_specs=[any_spec] * 2,
        out_specs=(any_spec, any_spec),
        scratch_shapes=[
            pltpu.VMEM(rows.shape, rows.dtype),
            pltpu.VMEM(cache.shape, cache.dtype),
            pltpu.SemaphoreType.DMA((5,)),
            pltpu.SemaphoreType.DMA((5,)),
        ],
    )(rows, cache)


def body(
    activations,
    slot_segment,
    attn_norm_gain,
    attn_norm_bias,
    mlp_norm_gain,
    mlp_norm_bias,
    qkv_weight,
    dense_weight,
    fc_weight,
    proj_weight,
):
    slots, width = activations.shape
    groups = lax.axis_size("req")
    members = lax.axis_size("mlp")
    model = qkv_weight.shape[0]
    pieces = len(PIECES)
    rows = max(size for _, size in PIECES)
    half = slots // 2
    kv_w = dense_weight.shape[0]
    ff = fc_weight.shape[1]
    live_rows = slots // 2
    chips = members // 2
    dma = pltpu.SemaphoreType.DMA
    any_spec = pl.BlockSpec(memory_space=pl.ANY)
    vmem_spec = pl.BlockSpec(memory_space=pltpu.VMEM)
    vecs = [
        v.reshape(model // 128, 128)
        for v in (attn_norm_gain, attn_norm_bias, mlp_norm_gain, mlp_norm_bias)
    ]
    results = pl.pallas_call(
        functools.partial(layer_kernel, groups, members),
        name="layer",
        out_shape=(
            jax.ShapeDtypeStruct((slots, width), F32),
            jax.ShapeDtypeStruct((2, live_rows, kv_w), BF16),
        ),
        in_specs=[any_spec] + [vmem_spec] * 5 + [any_spec] * 4,
        out_specs=(any_spec, any_spec),
        scratch_shapes=[
            pltpu.VMEM((members, slots, width), BF16),
            pltpu.VMEM(qkv_weight.shape, BF16),
            pltpu.VMEM(fc_weight.shape, BF16),
            pltpu.VMEM((kv_w + ff, model), BF16),
            pltpu.VMEM((rows, model), BF16),
            pltpu.VMEM((rows, model), BF16),
            pltpu.VMEM((4, members, width), F32),
            pltpu.VMEM((slots, 128), F32),
            pltpu.VMEM((3, slots, 128), F32),
            pltpu.VMEM((rows, kv_w), BF16),
            pltpu.VMEM((slots, 2 * kv_w), BF16),
            pltpu.VMEM((rows, kv_w + ff), BF16),
            pltpu.VMEM((slots, 2 * kv_w), BF16),
            pltpu.VMEM((slots, 2 * kv_w), BF16),
            pltpu.VMEM((8, 128), F32),
            pltpu.VMEM((groups, 8, 128), F32),
            pltpu.VMEM((chips, slots, width), BF16),
            pltpu.VMEM((chips, slots, width), BF16),
            pltpu.VMEM((chips, slots, width), F32),
            pltpu.VMEM((2, half, width), BF16),
            pltpu.VMEM((2, half, width), BF16),
            pltpu.VMEM((2, 2, half, width), BF16),
            pltpu.VMEM((2, 2, half, width), BF16),
            pltpu.VMEM((3, rows, 128), F32),
            pltpu.VMEM((slots, width), F32),
            pltpu.VMEM((2, live_rows, kv_w), BF16),
            dma((pieces + 1,)),
            dma((4,)),
            dma((pieces,)),
            dma((pieces, 11)),
            dma((pieces, 11)),
            dma((groups,)),
            dma((groups,)),
            dma((groups,)),
            dma((groups,)),
            dma((pieces, chips)),
            dma((pieces, chips)),
            dma((pieces, 2)),
            dma((pieces, 2)),
            dma((pieces, 2, 2)),
            dma((pieces, 2, 2)),
        ],
        compiler_params=pltpu.CompilerParams(
            collective_id=0, has_side_effects=True, vmem_limit_bytes=62 * 1024 * 1024
        ),
    )(
        activations,
        slot_segment.reshape(slots // 128, 128),
        *vecs,
        qkv_weight,
        dense_weight,
        fc_weight,
        proj_weight,
    )
    return deliver(*results)


def solution(mesh):
    placed = (
        P("req", "mlp"),
        P("req"),
        P(),
        P(),
        P(),
        P(),
        P(None, "mlp"),
        P("mlp", None),
        P(None, "mlp"),
        P("mlp", None),
    )
    return jax.shard_map(
        body,
        mesh=mesh,
        in_specs=placed,
        out_specs=(P("req", "mlp"), P(None, "req", "mlp")),
        check_vma=False,
    )
```
